32 devices in a mesh: grp: 4 (over y, x), dev: 8 (over z, core).
Axes of the slice: x: 2, y: 2, z: 4, core: 2. Of those that a mesh axis runs over, the one named last changes fastest.
Arguments:
- pool_latent: bfloat16 [512, 256, 512], P(('grp', 'dev')), may hold values from -6 to 6
- pool_rope: bfloat16 [512, 64, 256], P(('grp', 'dev')), may hold values from -6 to 6
- q_nope: bfloat16 [1024, 16384], P(None, 'dev'), may hold values from -6 to 6
- q_rope: bfloat16 [1024, 8192], P(None, 'dev'), may hold values from -9 to 9
- w_uk: bfloat16 [512, 16384], P(None, 'dev'), may hold values from -0.25 to 0.25
- w_uv: bfloat16 [512, 16384], P(None, 'dev'), may hold values from -0.25 to 0.25
- w_o: bfloat16 [16384, 7168], P('dev'), may hold values from -0.046875 to 0.046875
- block_table: int32 [64, 8], replicated, may hold values from 0 to 511, as said below
- lengths: int32 [64], replicated, may hold values from 2 to 2048, as said below
- preempted: int32 [32], replicated, may hold values from 0 to 63, as said below
- assignment: int32 [32], replicated, may hold values from 0 to 3, as said below
Outputs:
- mixed: bfloat16 [1024, 7168], P('grp', 'dev')
The draws below stay inside these ranges and needn't reach their ends.
Inputs may be any that keep to these rules, and one draw needn't show every extreme that they name: `preempted`: distinct slots. `assignment`: each group receives exactly 8 requests. `block_table`: every page number 0 to 511 appears exactly once in the table; page p lies on the device with index p // 16 along grp+dev, at position p % 16 there. For every group and every index along dev, exactly 8 of the pages listed for the slots of that group's requests lie on devices with that index along dev. `lengths`: in every draw all requests of one group hold more than (7) * 256 tokens.
All inputs are finite; a program needn't handle non-finite values.
Results may differ from the reference program's by a relative error of at most 0.015.
Values may be sent and summed in bfloat16 or wider, within the bound.
A program may use at most 256 MiB of HBM per device.

```python
import math
import jax
import jax.numpy as jnp
from jax import lax

D = 7168
H = 128
DC = 512
DR = 64
DN = 128
DV = 128
BLK = 256
NB = 8
REQ_G = 8
QR = 32
REQ = 32
SLOTS = 64
QROWS = 1024
GB = 64
C2 = 8
PG_DEV = 16
PAGES = 512


def layout_tables(key):
    groups = REQ // REQ_G
    columns = GB // C2
    slot_order = jax.random.permutation(jax.random.fold_in(key, 11), SLOTS).astype(jnp.int32)
    chosen = slot_order[:REQ]
    spare = slot_order[REQ:]
    group_order = jax.random.permutation(jax.random.fold_in(key, 12), REQ).astype(jnp.int32)
    assignment = group_order // REQ_G
    rank = group_order % REQ_G
    heavy = jax.random.randint(jax.random.fold_in(key, 13), (), 0, groups, dtype=jnp.int32)
    free_len = jax.random.randint(jax.random.fold_in(key, 14), (SLOTS,), 2, NB * BLK + 1, dtype=jnp.int32)
    full_len = jax.random.randint(jax.random.fold_in(key, 15), (REQ,), (NB - 1) * BLK + 1, NB * BLK + 1, dtype=jnp.int32)
    request_len = jnp.where(assignment == heavy, full_len, free_len[chosen])
    lengths = free_len.at[chosen].set(request_len)
    column_slots = groups * PG_DEV
    column_keys = jax.random.split(jax.random.fold_in(key, 16), columns)
    perms = jax.vmap(lambda k: jax.random.permutation(k, column_slots))(column_keys).astype(jnp.int32)
    row_of = perms // PG_DEV
    unit_of = perms % PG_DEV
    column_ids = jnp.arange(columns, dtype=jnp.int32)[:, None]
    page_at = (row_of * columns + column_ids) * PG_DEV + unit_of
    block_ids = jnp.arange(NB, dtype=jnp.int32)[None, :]
    k_chosen = rank[:, None] * NB + block_ids
    chosen_pages = page_at[k_chosen % columns, assignment[:, None] * C2 + k_chosen // columns]
    k_spare = jnp.arange(REQ, dtype=jnp.int32)[:, None] * NB + block_ids
    spare_pages = page_at[k_spare % columns, groups * C2 + k_spare // columns]
    table = jnp.zeros((SLOTS, NB), jnp.int32).at[chosen].set(chosen_pages).at[spare].set(spare_pages)
    return (chosen, assignment, lengths, table)


def draw_block_table(key, part):
    return layout_tables(key)[3]


def draw_lengths(key, part):
    return layout_tables(key)[2]


def draw_preempted(key, part):
    return layout_tables(key)[0]


def draw_assignment(key, part):
    return layout_tables(key)[1]


def draw_pool_rope(key, part):
    base = jnp.clip(jax.random.normal(jax.random.fold_in(key, 22), (PAGES, DR, BLK), jnp.float32), -6.0, 6.0)
    return base.astype(jnp.bfloat16)


def draw_q_rope(key, part):
    base = jnp.clip(jax.random.normal(jax.random.fold_in(key, 23), (QROWS, H * DR), jnp.float32), -8.0, 8.0)
    return base.astype(jnp.bfloat16)


def shard_levels(rng, extent, cuts, low, largest):
    def one(axis_at, shards_of):
        draws = jax.random.uniform(jax.random.fold_in(jax.random.fold_in(rng, 6), axis_at), (shards_of,), jnp.float32, low / len(cuts), largest / len(cuts))
        return jnp.repeat(jnp.exp(draws), extent[axis_at] // shards_of).reshape((-1,) + (1,) * (len(extent) - axis_at - 1))

    gain = one(*cuts[0])
    for cut in cuts[1:]:
        gain = gain * one(*cut)
    return gain


def normal_values(own_key, dims, deviation, most, cuts=(), kind=jnp.bfloat16):
    drawn = jax.random.normal(own_key, dims, jnp.float32) * deviation
    if len(cuts) > 0:
        drawn = shard_levels(own_key, dims, cuts, -0.22, 0.18) * drawn
    return jnp.clip(drawn, min=-most, max=most).astype(kind)


def setup_inputs(seed: int = 0) -> dict:
    keys = jax.random.split(jax.random.key(seed), 12)
    return {
        "pool_latent": normal_values(keys[0], (PAGES, BLK, DC), 1.0, 6.0, ((0, 32),)),
        "pool_rope": draw_pool_rope(jax.random.fold_in(keys[11], 71), 0),
        "q_nope": normal_values(keys[2], (QROWS, H * DN), 1.0, 6.0, ((1, 8),)),
        "q_rope": draw_q_rope(jax.random.fold_in(keys[11], 71), 0),
        "w_uk": normal_values(keys[4], (DC, H * DN), DC ** -0.5, 0.25, ((1, 8),)),
        "w_uv": normal_values(keys[5], (DC, H * DV), DC ** -0.5, 0.25, ((1, 8),)),
        "w_o": normal_values(keys[6], (H * DV, D), (H * DV) ** -0.5, 0.046875, ((0, 8),)),
        "block_table": draw_block_table(jax.random.fold_in(keys[11], 71), 0),
        "lengths": draw_lengths(jax.random.fold_in(keys[11], 71), 0),
        "preempted": draw_preempted(jax.random.fold_in(keys[11], 71), 0),
        "assignment": draw_assignment(jax.random.fold_in(keys[11], 71), 0),
    }


NEG = -1e+30

def reference(pool_latent, pool_rope, q_nope, q_rope, w_uk, w_uv, w_o, block_table, lengths, preempted, assignment):
    scale = 1.0 / math.sqrt(DN + DR)
    req_ids = jnp.arange(REQ, dtype=jnp.int32)
    earlier = (assignment[:, None] == assignment[None, :]) & (req_ids[None, :] < req_ids[:, None])
    rank = lax.optimization_barrier(jnp.sum(earlier.astype(jnp.int32), axis=1))
    dest = (assignment * REQ_G + rank).astype(jnp.int32)
    w_key = w_uk.astype(jnp.float32).reshape(DC, H, DN)
    w_val = w_uv.astype(jnp.float32).reshape(DC, H, DV)
    positions = jnp.arange(NB * BLK, dtype=jnp.int32)

    def one_request(index):
        slot = preempted[index]
        pages = block_table[slot]
        length = lengths[slot]
        latent = pool_latent[pages].reshape(NB * BLK, DC).astype(jnp.float32)
        rope = jnp.transpose(pool_rope[pages], (0, 2, 1)).reshape(NB * BLK, DR).astype(jnp.float32)
        start = (index * QR).astype(jnp.int32)
        query_lo = lax.dynamic_slice_in_dim(q_nope, start, QR, 0).astype(jnp.float32).reshape(QR, H, DN)
        query_hi = lax.dynamic_slice_in_dim(q_rope, start, QR, 0).astype(jnp.float32).reshape(QR, H, DR)
        q_lat = jnp.einsum('thn,chn->thc', query_lo, w_key)
        q_lat = lax.optimization_barrier(q_lat.astype(jnp.bfloat16)).astype(jnp.float32)
        score = jnp.einsum('thc,kc->thk', q_lat, latent) + jnp.einsum('thr,kr->thk', query_hi, rope)
        score = score * scale
        valid = positions[None, None, :] < length
        score = jnp.where(valid, score, NEG)
        top = lax.optimization_barrier(jnp.max(score, axis=2, keepdims=True))
        expo = jnp.where(valid, jnp.exp(score - top), 0.0)
        total = lax.optimization_barrier(jnp.sum(expo, axis=2))
        weights = lax.optimization_barrier(expo.astype(jnp.bfloat16)).astype(jnp.float32)
        o_lat = jnp.einsum('thk,kc->thc', weights, latent) / total[:, :, None]
        o_lat = lax.optimization_barrier(o_lat.astype(jnp.bfloat16)).astype(jnp.float32)
        heads = jnp.einsum('thc,chv->thv', o_lat, w_val).astype(jnp.bfloat16)
        return heads.reshape(QR, H * DV)
    heads_all = lax.map(one_request, req_ids)
    source = jnp.zeros((REQ,), jnp.int32).at[dest].set(req_ids)
    ordered = heads_all[source].reshape(QROWS, H * DV)
    return jnp.dot(ordered, w_o, preferred_element_type=jnp.float32).astype(jnp.bfloat16)
```

```python
import functools
import math

import jax
import jax.numpy as jnp
from jax import lax
from jax.experimental import pallas as pl
from jax.experimental.pallas import tpu as pltpu
from jax.sharding import PartitionSpec as P

DR = 64
DN = 128
DV = 128
CHUNKS = 2
ROWS = 256

NEG = -1e30


def choose(onehot, values):
    return jnp.sum(jnp.where(onehot, values, 0), axis=-1, dtype=jnp.int32)


def attend(first, last, offset, blocks, block, span, scale, where, sizes, *refs):
    q_ref, qr_ref = refs[:2]
    pages = refs[2 : 2 + blocks]
    refs = refs[2 + blocks :]
    if not first:
        acc_in, top_in, sum_in = refs[:3]
        refs = refs[3:]
    if last:
        out_ref = refs[0]
        refs = refs[1:]
    else:
        acc_out, top_out, sum_out = refs[:3]
        refs = refs[3:]
    lat, rope = refs
    width = lat.shape[1]
    heads, count, _ = q_ref.shape
    rope_width = rope.shape[0]
    fold = width // span
    depth = rope_width // fold
    for b in range(blocks):
        lat[b * span : (b + 1) * span, :] = pages[b][0, :span, :]
        for j in range(fold):
            rope[j * depth : (j + 1) * depth, b * span : (b + 1) * span] = pages[b][
                0, span:, j * span : (j + 1) * span
            ]
    length = sizes[pl.program_id(0)]
    token = lax.broadcasted_iota(jnp.int32, (1, blocks * span), 1)
    position = (token // span) * block + token % span + offset
    bias = jnp.where(position < length, 0.0, NEG)
    some = max(1, min(heads, ROWS // count))
    for h in range(0, heads, some):
        rows = some * count
        q = q_ref[h : h + some].reshape(rows, width)
        qr = qr_ref[h : h + some].reshape(rows, rope_width)
        score = lax.dot_general(
            q, lat[...], (((1,), (1,)), ((), ())), preferred_element_type=jnp.float32
        ) + jnp.dot(qr, rope[...], preferred_element_type=jnp.float32)
        score = score * scale + bias
        top = jnp.max(score, axis=1, keepdims=True)
        if not first:
            old = top_in[h : h + some].reshape(rows, 128)[:, :1]
            top = jnp.maximum(top, old)
        expo = jnp.exp(score - top)
        total = jnp.sum(expo, axis=1, keepdims=True)
        acc = jnp.dot(expo.astype(jnp.bfloat16), lat[...], preferred_element_type=jnp.float32)
        if not first:
            fade = jnp.exp(old - top)
            total = total + fade * sum_in[h : h + some].reshape(rows, 128)[:, :1]
            acc = acc + fade * acc_in[h : h + some].reshape(rows, width)
        if last:
            out_ref[h : h + some] = (acc / total).astype(out_ref.dtype).reshape(some, count, width)
        else:
            acc_out[h : h + some] = acc.reshape(some, count, width)
            top_out[h : h + some] = jnp.broadcast_to(top, (rows, 128)).reshape(some, count, 128)
            sum_out[h : h + some] = jnp.broadcast_to(total, (rows, 128)).reshape(some, count, 128)


def attention(state, q_lat, q_hi, pages, where, sizes, block, chunk, span, scale, count, blocks):
    heads, rows, width = q_lat.shape
    rope_width = q_hi.shape[2]
    requests = rows // count
    first, last = chunk == 0, chunk == CHUNKS - 1

    def rowspec(w):
        return pl.BlockSpec((heads, count, w), lambda r, *_: (0, r, 0))

    def pagespec(b):
        return pl.BlockSpec(
            (1,) + pages.shape[1:], lambda r, where, sizes: (where[r * blocks + b], 0, 0)
        )

    in_specs = [rowspec(width), rowspec(rope_width)] + [pagespec(b) for b in range(blocks)]
    if not first:
        in_specs += [rowspec(width), rowspec(128), rowspec(128)]
    if last:
        out_specs = rowspec(width)
        out_shape = jax.ShapeDtypeStruct((heads, rows, width), jnp.bfloat16)
    else:
        out_specs = [rowspec(width), rowspec(128), rowspec(128)]
        out_shape = [
            jax.ShapeDtypeStruct((heads, rows, w), jnp.float32) for w in (width, 128, 128)
        ]
    tokens = blocks * span
    return pl.pallas_call(
        functools.partial(attend, first, last, chunk * span, blocks, block, span, scale),
        grid_spec=pltpu.PrefetchScalarGridSpec(
            num_scalar_prefetch=2,
            grid=(requests,),
            in_specs=in_specs,
            out_specs=out_specs,
            scratch_shapes=[
                pltpu.VMEM((tokens, width), jnp.bfloat16),
                pltpu.VMEM((rope_width, tokens), jnp.bfloat16),
            ],
        ),
        out_shape=out_shape,
        cost_estimate=pl.CostEstimate(
            flops=2 * heads * rows * tokens * (2 * width + rope_width),
            bytes_accessed=pages.size * 2 + heads * rows * width * 8,
            transcendentals=heads * rows * tokens,
        ),
        compiler_params=pltpu.CompilerParams(vmem_limit_bytes=48 * 1024 * 1024),
        name=f"attend{chunk}",
    )(where, sizes, q_lat, q_hi, *([pages] * blocks), *state)


def local(
    pool_latent,
    pool_rope,
    q_nope,
    q_rope,
    w_uk,
    w_uv,
    w_o,
    block_table,
    lengths,
    preempted,
    assignment,
):
    groups = lax.axis_size("grp")
    columns = lax.axis_size("dev")
    group = lax.axis_index("grp")
    column = lax.axis_index("dev")
    pages_dev, block, latent_width = pool_latent.shape
    rope_width = pool_rope.shape[1]
    requests = preempted.shape[0]
    slots, blocks = block_table.shape
    per_group = requests // groups
    group_pages = per_group * blocks
    per_column = group_pages // columns
    query_rows = q_nope.shape[0] // requests
    heads_dev = q_rope.shape[1] // rope_width
    scale = 1.0 / math.sqrt(DN + DR)
    span = block // CHUNKS
    fold = latent_width // span
    entries = requests * blocks

    hot = preempted[:, None] == jnp.arange(slots, dtype=jnp.int32)[None, :]
    slot_pages = choose(hot[:, None, :], block_table.T[None, :, :])
    slot_len = choose(hot, lengths[None, :])
    req_ids = jnp.arange(requests, dtype=jnp.int32)
    earlier = (assignment[:, None] == assignment[None, :]) & (req_ids[None, :] < req_ids[:, None])
    rank = jnp.sum(earlier.astype(jnp.int32), axis=1)
    block_ids = jnp.arange(blocks, dtype=jnp.int32)
    page = slot_pages.reshape(entries)
    used = (block_ids[None, :] * block < slot_len[:, None]).reshape(entries)
    entry_group = jnp.broadcast_to(assignment[:, None], (requests, blocks)).reshape(entries)
    entry_place = jnp.broadcast_to(rank[:, None] * blocks, (requests, blocks)).reshape(
        entries
    ) + jnp.broadcast_to(block_ids[None, :], (requests, blocks)).reshape(entries)
    ids = jnp.arange(entries, dtype=jnp.int32)
    holder = page // pages_dev
    entry_row = holder // columns
    entry_col = holder % columns
    entry_local = page % pages_dev
    ahead = ids[None, :] < ids[:, None]
    same = (entry_col * groups + entry_group)[:, None] == (entry_col * groups + entry_group)[None, :]
    entry_slot = jnp.sum((same & ahead).astype(jnp.int32), axis=1)
    same_row = same & (entry_row[:, None] == entry_row[None, :]) & used[None, :]
    entry_turn = jnp.sum((same_row & ahead).astype(jnp.int32), axis=1)
    deepest = jnp.max(jnp.where(used, entry_turn + 1, 0))

    sending = used & (entry_row == group) & (entry_col == column)
    mine = used & (entry_group == group) & (entry_col == column)
    column_ids = jnp.arange(per_column, dtype=jnp.int32)
    mine_hot = mine[None, :] & (entry_slot[None, :] == column_ids[:, None])
    from_row = choose(mine_hot, entry_row[None, :])
    from_turn = choose(mine_hot, entry_turn[None, :])
    in_group = entry_group == group
    place_ids = jnp.arange(group_pages, dtype=jnp.int32)
    where = choose(
        in_group[None, :] & (entry_place[None, :] == place_ids[:, None]),
        (entry_col * per_column + entry_slot)[None, :],
    )
    group_ids = jnp.arange(per_group, dtype=jnp.int32)
    member_hot = (assignment == group)[None, :] & (rank[None, :] == group_ids[:, None])
    members = choose(member_hot, req_ids[None, :])
    sizes = choose(member_hot, slot_len[None, :])

    def exchange(chunk, capacity, _):
        turns = jnp.arange(groups * capacity, dtype=jnp.int32)
        target = jnp.where(
            sending & (entry_turn < capacity), entry_group * capacity + entry_turn, -1
        )
        index = choose(target[None, :] == turns[:, None], entry_local[None, :])
        part = slice(chunk * span, (chunk + 1) * span)
        rope = pool_rope[:, :, part]
        packed = jnp.concatenate(
            [
                pool_latent[:, part, :],
                jnp.concatenate(jnp.split(rope, fold, axis=1), axis=2),
            ],
            axis=1,
        )
        out = packed[index]
        got = lax.all_to_all(out, "grp", split_axis=0, concat_axis=0, tiled=True)
        return got[from_row * capacity + from_turn]

    capacities = [c for c in (4, 5, 6) if c < per_column] + [per_column]
    branch = jnp.sum(jnp.array([deepest > c for c in capacities[:-1]], jnp.int32)) if len(
        capacities
    ) > 1 else None

    own = []
    for chunk in range(CHUNKS):
        forms = [functools.partial(exchange, chunk, c) for c in capacities]
        own.append(forms[0](0) if branch is None else lax.switch(branch, forms, jnp.int32(0)))
    gathered = [lax.all_gather(o, "dev", axis=0, tiled=True) for o in own]

    query_lo = q_nope.reshape(requests, query_rows, heads_dev * DN)[members]
    query_hi = q_rope.reshape(requests, query_rows, heads_dev * rope_width)[members]
    query_lo = query_lo.reshape(per_group * query_rows, heads_dev, DN)
    query_hi = query_hi.reshape(per_group * query_rows, heads_dev, rope_width).transpose(1, 0, 2)
    w_key = w_uk.reshape(latent_width, heads_dev, DN)
    q_lat = jnp.einsum("qhn,chn->hqc", query_lo, w_key, preferred_element_type=jnp.float32).astype(
        jnp.bfloat16
    )

    state = ()
    for chunk in range(CHUNKS):
        state = attention(
            state,
            q_lat,
            query_hi,
            gathered[chunk],
            where,
            sizes,
            block,
            chunk,
            span,
            scale,
            query_rows,
            blocks,
        )
    o_lat = state
    w_val = w_uv.reshape(latent_width, heads_dev, DV)
    heads_out = jnp.einsum("hqc,chv->qhv", o_lat, w_val, preferred_element_type=jnp.float32).astype(
        jnp.bfloat16
    )
    heads_out = heads_out.reshape(per_group * query_rows, heads_dev * DV)
    mixed = lax.psum_scatter(
        lax.dot_general(
            w_o, heads_out, (((0,), (1,)), ((), ())), preferred_element_type=jnp.float32
        ).astype(jnp.bfloat16),
        "dev",
        scatter_dimension=0,
        tiled=True,
    )
    return mixed.T


def solution(mesh):
    in_specs = (
        P(("grp", "dev"), None, None),
        P(("grp", "dev"), None, None),
        P(None, "dev"),
        P(None, "dev"),
        P(None, "dev"),
        P(None, "dev"),
        P("dev", None),
        P(),
        P(),
        P(),
        P(),
    )
    out_specs = P("grp", "dev")
    return jax.shard_map(local, mesh=mesh, in_specs=in_specs, out_specs=out_specs, check_vma=False)
```

```python
import functools
import math

import jax
import jax.numpy as jnp
from jax import lax
from jax.experimental import pallas as pl
from jax.experimental.pallas import tpu as pltpu
from jax.sharding import PartitionSpec as P

DR = 64
DN = 128
DV = 128
CHUNKS = 2
ROWS = 256

NEG = -1e30


def choose(onehot, values):
    return jnp.sum(jnp.where(onehot, values, 0), axis=-1, dtype=jnp.int32)


def attend(first, last, offset, blocks, block, span, scale, where, sizes, *refs):
    q_ref, qr_ref = refs[:2]
    pages = refs[2 : 2 + blocks]
    refs = refs[2 + blocks :]
    if not first:
        acc_in, top_in, sum_in = refs[:3]
        refs = refs[3:]
    if last:
        out_ref = refs[0]
        refs = refs[1:]
    else:
        acc_out, top_out, sum_out = refs[:3]
        refs = refs[3:]
    lat, rope = refs
    width = lat.shape[1]
    heads, count, _ = q_ref.shape
    rope_width = rope.shape[0]
    fold = width // span
    depth = rope_width // fold
    for b in range(blocks):
        lat[b * span : (b + 1) * span, :] = pages[b][0, :span, :]
        for j in range(fold):
            rope[j * depth : (j + 1) * depth, b * span : (b + 1) * span] = pages[b][
                0, span:, j * span : (j + 1) * span
            ]
    length = sizes[pl.program_id(0)]
    token = lax.broadcasted_iota(jnp.int32, (1, blocks * span), 1)
    position = (token // span) * block + token % span + offset
    bias = jnp.where(position < length, 0.0, NEG)
    some = max(1, min(heads, ROWS // count))
    for h in range(0, heads, some):
        rows = some * count
        q = q_ref[h : h + some].reshape(rows, width)
        qr = qr_ref[h : h + some].reshape(rows, rope_width)
        score = lax.dot_general(
            q, lat[...], (((1,), (1,)), ((), ())), preferred_element_type=jnp.float32
        ) + jnp.dot(qr, rope[...], preferred_element_type=jnp.float32)
        score = score * scale + bias
        top = jnp.max(score, axis=1, keepdims=True)
        if not first:
            old = top_in[h : h + some].reshape(rows, 128)[:, :1]
            top = jnp.maximum(top, old)
        expo = jnp.exp(score - top)
        total = jnp.sum(expo, axis=1, keepdims=True)
        acc = jnp.dot(expo.astype(jnp.bfloat16), lat[...], preferred_element_type=jnp.float32)
        if not first:
            fade = jnp.exp(old - top)
            total = total + fade * sum_in[h : h + some].reshape(rows, 128)[:, :1]
            acc = acc + fade * acc_in[h : h + some].reshape(rows, width)
        if last:
            out_ref[h : h + some] = (acc / total).astype(out_ref.dtype).reshape(some, count, width)
        else:
            acc_out[h : h + some] = acc.reshape(some, count, width)
            top_out[h : h + some] = jnp.broadcast_to(top, (rows, 128)).reshape(some, count, 128)
            sum_out[h : h + some] = jnp.broadcast_to(total, (rows, 128)).reshape(some, count, 128)


def attention(state, q_lat, q_hi, pages, where, sizes, block, chunk, span, scale, count, blocks):
    heads, rows, width = q_lat.shape
    rope_width = q_hi.shape[2]
    requests = rows // count
    first, last = chunk == 0, chunk == CHUNKS - 1

    def rowspec(w):
        return pl.BlockSpec((heads, count, w), lambda r, *_: (0, r, 0))

    def pagespec(b):
        return pl.BlockSpec(
            (1,) + pages.shape[1:], lambda r, where, sizes: (where[r * blocks + b], 0, 0)
        )

    in_specs = [rowspec(width), rowspec(rope_width)] + [pagespec(b) for b in range(blocks)]
    if not first:
        in_specs += [rowspec(width), rowspec(128), rowspec(128)]
    if last:
        out_specs = rowspec(width)
        out_shape = jax.ShapeDtypeStruct((heads, rows, width), jnp.bfloat16)
    else:
        out_specs = [rowspec(width), rowspec(128), rowspec(128)]
        out_shape = [
            jax.ShapeDtypeStruct((heads, rows, w), jnp.float32) for w in (width, 128, 128)
        ]
    tokens = blocks * span
    return pl.pallas_call(
        functools.partial(attend, first, last, chunk * span, blocks, block, span, scale),
        grid_spec=pltpu.PrefetchScalarGridSpec(
            num_scalar_prefetch=2,
            grid=(requests,),
            in_specs=in_specs,
            out_specs=out_specs,
            scratch_shapes=[
                pltpu.VMEM((tokens, width), jnp.bfloat16),
                pltpu.VMEM((rope_width, tokens), jnp.bfloat16),
            ],
        ),
        out_shape=out_shape,
        cost_estimate=pl.CostEstimate(
            flops=2 * heads * rows * tokens * (2 * width + rope_width),
            bytes_accessed=pages.size * 2 + heads * rows * width * 8,
            transcendentals=heads * rows * tokens,
        ),
        compiler_params=pltpu.CompilerParams(vmem_limit_bytes=48 * 1024 * 1024),
        name=f"attend{chunk}",
    )(where, sizes, q_lat, q_hi, *([pages] * blocks), *state)


def local(
    pool_latent,
    pool_rope,
    q_nope,
    q_rope,
    w_uk,
    w_uv,
    w_o,
    block_table,
    lengths,
    preempted,
    assignment,
):
    groups = lax.axis_size("grp")
    columns = lax.axis_size("dev")
    group = lax.axis_index("grp")
    column = lax.axis_index("dev")
    pages_dev, block, latent_width = pool_latent.shape
    rope_width = pool_rope.shape[1]
    requests = preempted.shape[0]
    slots, blocks = block_table.shape
    per_group = requests // groups
    group_pages = per_group * blocks
    per_column = group_pages // columns
    query_rows = q_nope.shape[0] // requests
    heads_dev = q_rope.shape[1] // rope_width
    scale = 1.0 / math.sqrt(DN + DR)
    span = block // CHUNKS
    fold = latent_width // span
    entries = requests * blocks

    hot = preempted[:, None] == jnp.arange(slots, dtype=jnp.int32)[None, :]
    slot_pages = choose(hot[:, None, :], block_table.T[None, :, :])
    slot_len = choose(hot, lengths[None, :])
    req_ids = jnp.arange(requests, dtype=jnp.int32)
    earlier = (assignment[:, None] == assignment[None, :]) & (req_ids[None, :] < req_ids[:, None])
    rank = jnp.sum(earlier.astype(jnp.int32), axis=1)
    block_ids = jnp.arange(blocks, dtype=jnp.int32)
    page = slot_pages.reshape(entries)
    used = (block_ids[None, :] * block < slot_len[:, None]).reshape(entries)
    entry_group = jnp.broadcast_to(assignment[:, None], (requests, blocks)).reshape(entries)
    entry_place = jnp.broadcast_to(rank[:, None] * blocks, (requests, blocks)).reshape(
        entries
    ) + jnp.broadcast_to(block_ids[None, :], (requests, blocks)).reshape(entries)
    ids = jnp.arange(entries, dtype=jnp.int32)
    holder = page // pages_dev
    entry_row = holder // columns
    entry_col = holder % columns
    entry_local = page % pages_dev
    ahead = ids[None, :] < ids[:, None]
    same = (entry_col * groups + entry_group)[:, None] == (entry_col * groups + entry_group)[None, :]
    entry_slot = jnp.sum((same & ahead).astype(jnp.int32), axis=1)
    same_row = same & (entry_row[:, None] == entry_row[None, :]) & used[None, :]
    entry_turn = jnp.sum((same_row & ahead).astype(jnp.int32), axis=1)
    deepest = jnp.max(jnp.where(used, entry_turn + 1, 0))

    sending = used & (entry_row == group) & (entry_col == column)
    mine = used & (entry_group == group) & (entry_col == column)
    column_ids = jnp.arange(per_column, dtype=jnp.int32)
    mine_hot = mine[None, :] & (entry_slot[None, :] == column_ids[:, None])
    from_row = choose(mine_hot, entry_row[None, :])
    from_turn = choose(mine_hot, entry_turn[None, :])
    in_group = entry_group == group
    place_ids = jnp.arange(group_pages, dtype=jnp.int32)
    where = choose(
        in_group[None, :] & (entry_place[None, :] == place_ids[:, None]),
        (entry_col * per_column + entry_slot)[None, :],
    )
    group_ids = jnp.arange(per_group, dtype=jnp.int32)
    member_hot = (assignment == group)[None, :] & (rank[None, :] == group_ids[:, None])
    members = choose(member_hot, req_ids[None, :])
    sizes = choose(member_hot, slot_len[None, :])

    def exchange(chunk, capacity, _):
        turns = jnp.arange(groups * capacity, dtype=jnp.int32)
        target = jnp.where(
            sending & (entry_turn < capacity), entry_group * capacity + entry_turn, -1
        )
        index = choose(target[None, :] == turns[:, None], entry_local[None, :])
        part = slice(chunk * span, (chunk + 1) * span)
        rope = pool_rope[:, :, part]
        packed = jnp.concatenate(
            [
                pool_latent[:, part, :],
                jnp.concatenate(jnp.split(rope, fold, axis=1), axis=2),
            ],
            axis=1,
        )
        out = packed[index]
        got = lax.all_to_all(out, "grp", split_axis=0, concat_axis=0, tiled=True)
        return got[from_row * capacity + from_turn]

    capacities = [c for c in (4, 5, 6) if c < per_column] + [per_column]
    branch = jnp.sum(jnp.array([deepest > c for c in capacities[:-1]], jnp.int32)) if len(
        capacities
    ) > 1 else None

    own = []
    for chunk in range(CHUNKS):
        forms = [functools.partial(exchange, chunk, c) for c in capacities]
        own.append(forms[0](0) if branch is None else lax.switch(branch, forms, jnp.int32(0)))
    gathered = [lax.all_gather(o, "dev", axis=0, tiled=True) for o in own]

    query_lo = q_nope.reshape(requests, query_rows, heads_dev * DN)[members]
    query_hi = q_rope.reshape(requests, query_rows, heads_dev * rope_width)[members]
    query_lo = query_lo.reshape(per_group * query_rows, heads_dev, DN)
    query_hi = query_hi.reshape(per_group * query_rows, heads_dev, rope_width).transpose(1, 0, 2)
    w_key = w_uk.reshape(latent_width, heads_dev, DN)
    q_lat = jnp.einsum("qhn,chn->hqc", query_lo, w_key, preferred_element_type=jnp.float32).astype(
        jnp.bfloat16
    )

    state = ()
    for chunk in range(CHUNKS):
        state = attention(
            state,
            q_lat,
            query_hi,
            gathered[chunk],
            where,
            sizes,
            block,
            chunk,
            span,
            scale,
            query_rows,
            blocks,
        )
    o_lat = state
    w_val = w_uv.reshape(latent_width, heads_dev, DV)
    heads_out = jnp.einsum("hqc,chv->qhv", o_lat, w_val, preferred_element_type=jnp.float32).astype(
        jnp.bfloat16
    )
    heads_out = heads_out.reshape(per_group * query_rows, heads_dev * DV)
    w_out = w_o.reshape(w_o.shape[0], columns, w_o.shape[1] // columns)
    half = heads_out.shape[0] // 2
    mixed = []
    for part in (heads_out[:half], heads_out[half:]):
        share = jnp.einsum("rk,kcd->crd", part, w_out, preferred_element_type=jnp.float32)
        mixed.append(lax.psum_scatter(share.astype(jnp.bfloat16), "dev", scatter_dimension=0))
    return jnp.concatenate(mixed, axis=0)


def solution(mesh):
    in_specs = (
        P(("grp", "dev"), None, None),
        P(("grp", "dev"), None, None),
        P(None, "dev"),
        P(None, "dev"),
        P(None, "dev"),
        P(None, "dev"),
        P("dev", None),
        P(),
        P(),
        P(),
        P(),
    )
    out_specs = P("grp", "dev")
    return jax.shard_map(local, mesh=mesh, in_specs=in_specs, out_specs=out_specs, check_vma=False)
```
